32 devices in a mesh: groups: 2 (over x), tokens: 16 (over z, y, core).
Axes of the slice: x: 2, y: 2, z: 4, core: 2. Of those that a mesh axis runs over, the one named last changes fastest.
Arguments:
- text_query: bfloat16 [256, 2, 1280], P(('groups', 'tokens')), parts along dimension 0, may hold values from -6 to 6
- frame_key: bfloat16 [16384, 2, 1280], P(('groups', 'tokens')), parts along dimension 0, may hold values from -6 to 6
- frame_value: bfloat16 [16384, 2560], P(('groups', 'tokens')), parts along dimension 0, may hold values from -6 to 6
- forward_out: bfloat16 [256, 2, 2560], P(('groups', 'tokens')), parts along dimension 0, may hold values from -3 to 3
- out_grad: bfloat16 [256, 2560], P(('groups', 'tokens')), parts along dimension 0, may hold values from -1536 to 1536
- log_norms: float32 [256, 2, 10], P(('groups', 'tokens')), parts along dimension 0, as said below
- lambdas: float32 [10], replicated, may hold values from 0.2 to 0.8
- visits: int32 [32, 12], P('groups'), parts along dimension 0, may hold values from 0 to 15, all different within a row; in each aligned block of 16 rows (0 to 15, 16 to 31, ...) at most 14 rows name the same one
- bounds: int32 [32], P('groups'), parts along dimension 0, may hold values from 2 to 6, as said below
- text_count: int32 [1], replicated, may hold values from 64 to 128
Outputs:
- query_grad: bfloat16 [256, 2, 1280], P(('groups', 'tokens')), parts along dimension 0
- key_grad: bfloat16 [16384, 2, 1280], P(('groups', 'tokens')), parts along dimension 0
- value_grad: bfloat16 [16384, 2560], P(('groups', 'tokens')), parts along dimension 0
The draws below stay inside these ranges and needn't reach their ends.
There are 2 independent parts, one for each index of `groups`. The reference program is written for one: setup_inputs(seed, part) draws one part's arguments, and reference() takes and returns one part's arrays. A program takes and returns all parts, laid end to end along the dimension named above; an argument that names none is the same for every part. Nothing has to cross between parts.
Inputs may be any that keep to these rules, and one draw needn't show every extreme that they name: `visits`: row b lists 6 frame shards for the first segment of text block b and then 6 for its second, all 12 different; every shard is listed by at most 14 blocks, a bound that some block reaches. Segment 1 of text block b begins at its row bounds[b]; some block has bounds 2 and some has 6, so no segment is longer than 6 rows. Text rows from text_count onward are padding in every group. `log_norms`: each entry lies within 1.5 of the logarithm of 3072.
All inputs are finite; a program needn't handle non-finite values.
Results may differ from the reference program's by a relative error of at most 0.005.
Values may be sent and summed in bfloat16 or wider, within the bound.
A program may use at most 128 MiB of HBM per device.

```python
import math
import jax
import jax.numpy as jnp
import numpy as np
from jax import lax

H = 10
KD = 128
VD = 256
F_DEV = 512
X_DEV = 8
VISITS = 6
MOST = 14
TEXT = 128
FRAMES = 8192
N_TOKENS = 16


def draw_log_norms(key, part):
    offset = math.log(VISITS * F_DEV)
    spread_draw = jax.random.uniform(key, (TEXT, 2, H), jnp.float32, 0.0, 1.0)
    return spread_draw + offset


def draw_bounds(key, part):
    base_key = jax.random.fold_in(key, 7)
    first_key, second_key = jax.random.split(base_key)
    lowest = X_DEV - 3 * X_DEV // 4
    highest = 3 * X_DEV // 4
    base = jax.random.randint(first_key, (N_TOKENS,), lowest, highest + 1, dtype=jnp.int32)
    order = jax.random.permutation(second_key, N_TOKENS)
    places = jnp.arange(N_TOKENS, dtype=jnp.int32)
    base = jnp.where(places == order[0], highest, base)
    base = jnp.where(places == order[1], lowest, base)
    return base.astype(jnp.int32)


def level_of(key, extent, cuts, least, largest):
    def one(dim, parts):
        heights = jax.random.uniform(jax.random.fold_in(jax.random.fold_in(key, 6), dim), (parts,), jnp.float32, least / len(cuts), largest / len(cuts))
        return jnp.repeat(jnp.exp(heights), extent[dim] // parts).reshape((-1,) + (1,) * (len(extent) - dim - 1))

    loudness = one(*cuts[0])
    for cut in cuts[1:]:
        loudness = loudness * one(*cut)
    return loudness


def shared_out(key, own, number, rows, count, top, limit, skew):
    sequence = jax.random.permutation(key, count)
    crowded, ordinary = load_shares(count, rows * top, limit, skew, True), load_shares(count, rows * top, limit, skew, False)
    places = jnp.arange(count)

    def named(sizes, rotation):
        used = int((sizes > 0).sum())
        fixed = max(1, used // 4)
        passed = fixed + (places - fixed + rotation * (used - fixed)) % max(1, count - fixed)
        return jnp.zeros((count,), jnp.int32).at[sequence[jnp.where(places < fixed, places, passed)]].set(jnp.asarray(sizes, jnp.int32))

    sizes = jnp.where(number % 4 == 0, named(crowded, number // 4), named(ordinary, number - number // 4 - 1))
    mixed = jax.random.permutation(jax.random.fold_in(own, 3), count)
    giver, sink = mixed[0:count // 2 * 2:2], mixed[1:count // 2 * 2:2]
    margin = jnp.minimum(sizes[giver] - 1, limit - sizes[sink]) // 2
    margin = jnp.where((giver == sequence[0]) | (sink == sequence[0]) | (sizes[sink] == 0), 0, jnp.maximum(margin, 0))
    passed = jax.random.randint(jax.random.fold_in(own, 4), (count // 2,), 0, 1 << 20) % (margin + 1)
    sizes = sizes.at[giver].add(-passed).at[sink].add(passed)
    items = jnp.searchsorted(jnp.cumsum(sizes), jnp.arange(rows * top), side="right").astype(jnp.int32)
    table = items.reshape(top, rows).T
    table = table[jax.random.permutation(jax.random.fold_in(own, 1), rows)]
    rotation = jax.random.randint(jax.random.fold_in(own, 2), (rows, 1), 0, top)
    return jnp.take_along_axis(table, (jnp.arange(top)[None, :] + rotation) % top, axis=1)


def load_shares(count, total, bound, slope, full):
    weights = [(1 << 20) // math.isqrt(standing ** slope) + 1 for standing in range(1, count + 1)]
    largest = bound if full else min(bound, max(-(-total // count), total * weights[0] // sum(weights)))
    least = 1 if total - largest >= count - 1 else 0
    given, surplus = [largest] + [least] * (count - 1), total - largest - least * (count - 1)
    while surplus > 0:
        movable = [i for i in range(1, count) if given[i] < largest] or [i for i in range(1, count) if given[i] < bound]
        pool, remaining = sum([weights[i] for i in movable]), surplus
        for i in movable:
            more = min(bound - given[i], max(1, remaining * weights[i] // pool), surplus)
            given[i] = given[i] + more
            surplus = surplus - more
    return np.array(given)


def gaussian(key, extent, scale, most, cuts=(), kind=jnp.bfloat16):
    result = scale * jax.random.normal(key, extent, jnp.float32)
    if cuts:
        result = result * level_of(key, extent, cuts, -0.22, 0.18)
    return jnp.clip(result, -most, most).astype(kind)


def setup_inputs(seed: int = 0, part: int = 0) -> dict:
    key_list = jax.random.split(jax.random.key(seed), 11)
    own_keys = jax.random.split(jax.random.fold_in(key_list[10], part), 11)
    text_query = gaussian(own_keys[0], (TEXT, 2, H * KD), 1.0, 6.0, ((0, 16),))
    frame_key = gaussian(own_keys[1], (FRAMES, 2, H * KD), 1.0, 6.0, ((0, 16),))
    frame_value = gaussian(own_keys[2], (FRAMES, H * VD), 1.0, 6.0, ((0, 16),))
    forward_out = gaussian(own_keys[3], (TEXT, 2, H * VD), 0.5, 3.0, ((0, 16),))
    out_grad = gaussian(own_keys[4], (TEXT, H * VD), 256.0, 1536.0, ((0, 16),))
    log_norms = draw_log_norms(jax.random.fold_in(jax.random.fold_in(key_list[10], part), 71), part)
    lambdas = jnp.clip(jnp.exp(jax.random.uniform(key_list[6], (H,), jnp.float32, math.log(0.2), math.log(0.8))), 0.2, 0.8)
    visits_keys = jax.random.split(jax.random.fold_in(own_keys[7], 1), N_TOKENS // N_TOKENS)
    visits_turns = jax.random.permutation(jax.random.fold_in(own_keys[7], 3), N_TOKENS // N_TOKENS)
    visits = jax.vmap(lambda own, number: shared_out(jax.random.fold_in(own_keys[7], 2), own, number, N_TOKENS, N_TOKENS, 2 * VISITS, MOST, 2))(visits_keys, visits_turns).reshape((N_TOKENS, 2 * VISITS))
    bounds = draw_bounds(jax.random.fold_in(jax.random.fold_in(key_list[10], part), 71), part)
    text_count = jax.random.randint(key_list[9], (1,), TEXT // 2, TEXT + 1).astype(jnp.int32)
    return {"text_query": text_query, "frame_key": frame_key, "frame_value": frame_value, "forward_out": forward_out, "out_grad": out_grad, "log_norms": log_norms, "lambdas": lambdas, "visits": visits, "bounds": bounds, "text_count": text_count}


def live_table(visits, bounds, text_count):
    row_index = jnp.arange(TEXT, dtype=jnp.int32)
    block_index = row_index // X_DEV
    in_second = (row_index - block_index * X_DEV) >= bounds[block_index]
    listed = visits.reshape(N_TOKENS, 2, VISITS)
    shard_index = jnp.arange(N_TOKENS, dtype=jnp.int32)
    hit_table = jnp.any(listed[:, :, :, None] == shard_index[None, None, None, :], axis=2)
    chosen = jnp.where(in_second[:, None], hit_table[block_index, 1], hit_table[block_index, 0])
    is_valid = row_index < text_count[0]
    return jnp.logical_and(chosen, is_valid[:, None]).astype(jnp.float32)


def reference(text_query, frame_key, frame_value, forward_out, out_grad, log_norms, lambdas, visits, bounds, text_count):
    live_full = jnp.repeat(live_table(visits, bounds, text_count), F_DEV, axis=1)
    score_scale = float(KD) ** -0.5
    query_heads = jnp.moveaxis(text_query.reshape(TEXT, 2, H, KD), 2, 0)
    key_heads = jnp.moveaxis(frame_key.reshape(FRAMES, 2, H, KD), 2, 0)
    value_heads = jnp.moveaxis(frame_value.reshape(FRAMES, H, VD), 1, 0)
    grad_heads = jnp.moveaxis(out_grad.reshape(TEXT, H, VD), 1, 0)
    out_heads = jnp.moveaxis(forward_out.reshape(TEXT, 2, H, VD), 2, 0)
    norm_heads = jnp.moveaxis(log_norms, 2, 0)

    def one_head(inputs):
        q_head, k_head, v_head, g_head, o_head, n_head, weight_two = inputs
        spread = jnp.dot(g_head, v_head.T, preferred_element_type=jnp.float32)
        g_wide = g_head.astype(jnp.float32)
        slope_one = jnp.sum(g_wide * o_head[:, 0].astype(jnp.float32), axis=1)
        slope_two = -weight_two * jnp.sum(g_wide * o_head[:, 1].astype(jnp.float32), axis=1)
        score_one = jnp.dot(q_head[:, 0], k_head[:, 0].T, preferred_element_type=jnp.float32) * score_scale
        score_two = jnp.dot(q_head[:, 1], k_head[:, 1].T, preferred_element_type=jnp.float32) * score_scale
        prob_one = live_full * jnp.exp(score_one - n_head[:, 0:1])
        prob_two = live_full * jnp.exp(score_two - n_head[:, 1:2])
        grad_one = (prob_one * (spread - slope_one[:, None])).astype(jnp.bfloat16)
        grad_two = (prob_two * (-weight_two * spread - slope_two[:, None])).astype(jnp.bfloat16)
        mixed_weight = (prob_one - weight_two * prob_two).astype(jnp.bfloat16)
        value_part = jnp.dot(mixed_weight.T, g_head, preferred_element_type=jnp.float32)
        key_part = jnp.stack([jnp.dot(grad_one.T, q_head[:, 0], preferred_element_type=jnp.float32),
                              jnp.dot(grad_two.T, q_head[:, 1], preferred_element_type=jnp.float32)], axis=1) * score_scale
        query_part = jnp.stack([jnp.dot(grad_one, k_head[:, 0], preferred_element_type=jnp.float32),
                                jnp.dot(grad_two, k_head[:, 1], preferred_element_type=jnp.float32)], axis=1) * score_scale
        return key_part, value_part, query_part

    key_all, value_all, query_all = lax.map(one_head, (query_heads, key_heads, value_heads, grad_heads, out_heads, norm_heads, lambdas))
    query_grad = jnp.moveaxis(query_all, 0, 2).reshape(TEXT, 2, H * KD).astype(jnp.bfloat16)
    key_grad = jnp.moveaxis(key_all, 0, 2).reshape(FRAMES, 2, H * KD).astype(jnp.bfloat16)
    value_grad = jnp.moveaxis(value_all, 0, 1).reshape(FRAMES, H * VD).astype(jnp.bfloat16)
    return (query_grad, key_grad, value_grad)
```

```python
import functools
import math

import jax
import jax.numpy as jnp
from jax import lax
from jax.experimental import pallas as pl
from jax.experimental.pallas import tpu as pltpu
from jax.sharding import PartitionSpec as P

MESH = pl.DeviceIdType.MESH
LOG2E = math.log2(math.e)
VMEM = pl.BlockSpec(memory_space=pltpu.VMEM)


def place(levels):
    me = lax.axis_index("tokens")
    bits = [(me // 2**k) % 2 for k in range(levels)]
    position = sum(bits[k] * 2 ** (levels - 1 - k) for k in range(levels))
    partners = []
    for s in range(levels):
        step = 2 ** (levels - 1 - s)
        partners.append(me + step - 2 * step * bits[levels - 1 - s])
    return position, partners


def greet(partners):
    barrier = pltpu.get_barrier_semaphore()
    for partner in partners:
        pl.semaphore_signal(barrier, inc=1, device_id={"tokens": partner}, device_id_type=MESH)
    pl.semaphore_wait(barrier, len(partners))


def gather_kernel(levels, rows_ref, stat_ref, rows_out, stat_out, send_sem, recv_sem, stat_send, stat_recv):
    position, partners = place(levels)
    chunks = rows_ref.shape[0]
    greet(partners)
    rows_out[position] = rows_ref[...]
    stat_out[position] = stat_ref[...]
    copies = {}
    for s in range(levels):
        size = 2**s
        start = position - position % size
        held = pl.ds(start, size)
        for c in range(chunks + 1):
            if s > 0:
                copies[s - 1, c].wait_recv()
            if c < chunks:
                view = rows_out.at[held, c]
                sems = (send_sem.at[s, c], recv_sem.at[s, c])
            else:
                view = stat_out.at[held]
                sems = (stat_send.at[s], stat_recv.at[s])
            copies[s, c] = pltpu.make_async_remote_copy(
                src_ref=view,
                dst_ref=view,
                send_sem=sems[0],
                recv_sem=sems[1],
                device_id={"tokens": partners[s]},
                device_id_type=MESH,
            )
            copies[s, c].start()
    for c in range(chunks + 1):
        copies[levels - 1, c].wait_recv()
    for copy in copies.values():
        copy.wait_send()


def gather_rows(count, rows, stats):
    levels = count.bit_length() - 1
    chunks = rows.shape[0]
    return pl.pallas_call(
        functools.partial(gather_kernel, levels),
        out_shape=(
            jax.ShapeDtypeStruct((count,) + rows.shape, rows.dtype),
            jax.ShapeDtypeStruct((count,) + stats.shape, stats.dtype),
        ),
        in_specs=[VMEM, VMEM],
        out_specs=(VMEM, VMEM),
        scratch_shapes=[
            pltpu.SemaphoreType.DMA((levels, chunks)),
            pltpu.SemaphoreType.DMA((levels, chunks)),
            pltpu.SemaphoreType.DMA((levels,)),
            pltpu.SemaphoreType.DMA((levels,)),
        ],
        compiler_params=pltpu.CompilerParams(
            collective_id=0, has_side_effects=True, vmem_limit_bytes=40 << 20
        ),
        name="gather_rows",
    )(rows, stats)


def head_kernel(lambda_ref, q_ref, g_ref, k_ref, v_ref, stat_ref, dq_ref, dk_ref, dv_ref, stat_t):
    head = pl.program_id(0)
    heads = pl.num_programs(0)
    me = lax.axis_index("tokens")
    blocks, _, block_rows, key_size = q_ref.shape
    rows = blocks * block_rows
    scale = float(key_size) ** -0.5

    @pl.when(head == 0)
    def _():
        stat_t[...] = stat_ref[...].reshape(rows, stat_ref.shape[2]).T

    def flat(x):
        return x.astype(jnp.float32).reshape(rows, x.shape[2]).astype(jnp.bfloat16)

    def row(i):
        return stat_t[pl.ds(i, 1), :]

    def dot(a, b, dims):
        return lax.dot_general(a, b, (dims, ((), ())), preferred_element_type=jnp.float32)

    weight_two = lambda_ref[head]
    live = row(4 * heads + me)
    g = flat(g_ref[:, 0])
    spread = dot(v_ref[...], g, ((1,), (1,)))
    probs = []
    for m in range(2):
        q = flat(q_ref[:, m])
        k = k_ref[m]
        score = dot(k, q, ((1,), (1,)))
        prob = live * jnp.exp2(score * (scale * LOG2E) - row(m * heads + head))
        coef_spread = spread if m == 0 else -weight_two * spread
        grad = (prob * (coef_spread - row((2 + m) * heads + head))).astype(jnp.bfloat16)
        probs.append(prob)
        dk_ref[m] = (dot(grad, q, ((1,), (0,))) * scale).astype(jnp.bfloat16)
        dq = dot(grad, k, ((0,), (0,))) * scale
        dq_ref[:, m] = dq.reshape(blocks, block_rows, key_size)
    mixed = (probs[0] - weight_two * probs[1]).astype(jnp.bfloat16)
    dv_ref[...] = dot(mixed, g, ((1,), (0,))).astype(jnp.bfloat16)


def heads_backward(rows, stats, keys, values, lambdas):
    heads = lambdas.shape[0]
    count, _, block_rows, width = rows.shape
    frames = keys.shape[1]
    key_size, value_size = width // heads, values.shape[1] // heads
    per_half = heads // 2
    return pl.pallas_call(
        head_kernel,
        out_shape=(
            jax.ShapeDtypeStruct((count, 2, block_rows, width), jnp.float32),
            jax.ShapeDtypeStruct(keys.shape, jnp.bfloat16),
            jax.ShapeDtypeStruct(values.shape, jnp.bfloat16),
        ),
        grid=(heads,),
        in_specs=[
            pl.BlockSpec(memory_space=pltpu.SMEM),
            pl.BlockSpec((count, 2, block_rows, key_size), lambda h: (0, 0, 0, h)),
            pl.BlockSpec((count, 1, block_rows, value_size), lambda h: (0, 2 + h // per_half, 0, h % per_half)),
            pl.BlockSpec((2, frames, key_size), lambda h: (0, 0, h)),
            pl.BlockSpec((frames, value_size), lambda h: (0, h)),
            pl.BlockSpec(stats.shape, lambda h: (0, 0, 0)),
        ],
        out_specs=(
            pl.BlockSpec((count, 2, block_rows, key_size), lambda h: (0, 0, 0, h)),
            pl.BlockSpec((2, frames, key_size), lambda h: (0, 0, h)),
            pl.BlockSpec((frames, value_size), lambda h: (0, h)),
        ),
        scratch_shapes=[pltpu.VMEM((stats.shape[2], count * block_rows), jnp.float32)],
        compiler_params=pltpu.CompilerParams(
            dimension_semantics=("arbitrary",), vmem_limit_bytes=48 << 20
        ),
        name="heads_backward",
    )(lambdas, rows, rows, keys, values, stats)


def sum_kernel(levels, chunks, part_ref, out_ref, total, sending, landed, send_sem, recv_sem):
    position, partners = place(levels)
    maps, width = part_ref.shape[1], part_ref.shape[3] // (chunks // part_ref.shape[1])
    per_map = chunks // maps
    greet(partners)
    copies = {}

    def cut(c):
        return (c // per_map, slice(None), slice((c % per_map) * width, (c % per_map + 1) * width))

    def send(s, c, source):
        size = 2**s
        bit = (position // size) % 2
        start = position - position % size + size - 2 * size * bit
        away = (pl.ds(start, size),) + cut(c)
        sending[away] = source[away].astype(sending.dtype)
        copies[s, c] = pltpu.make_async_remote_copy(
            src_ref=sending.at[away],
            dst_ref=landed.at[(pl.ds(size, size),) + cut(c)],
            send_sem=send_sem.at[s, c],
            recv_sem=recv_sem.at[s, c],
            device_id={"tokens": partners[s]},
            device_id_type=MESH,
        )
        copies[s, c].start()

    for c in range(chunks):
        send(levels - 1, c, part_ref)
    for s in range(levels - 1, -1, -1):
        size = 2**s
        source = part_ref if s == levels - 1 else total
        kept = pl.ds(position - position % size, size)
        for c in range(chunks):
            copies[s, c].wait_recv()
            got = landed[(pl.ds(size, size),) + cut(c)].astype(jnp.float32)
            new = source[(kept,) + cut(c)] + got
            if s > 0:
                total[(kept,) + cut(c)] = new
                send(s - 1, c, total)
            else:
                out_ref[cut(c)] = new[0].astype(out_ref.dtype)
    for copy in copies.values():
        copy.wait_send()


def sum_rows(part):
    count = part.shape[0]
    levels = count.bit_length() - 1
    chunks = 2 * part.shape[1]
    return pl.pallas_call(
        functools.partial(sum_kernel, levels, chunks),
        out_shape=jax.ShapeDtypeStruct(part.shape[1:], jnp.bfloat16),
        in_specs=[VMEM],
        out_specs=VMEM,
        scratch_shapes=[
            pltpu.VMEM(part.shape, jnp.float32),
            pltpu.VMEM(part.shape, jnp.bfloat16),
            pltpu.VMEM(part.shape, jnp.bfloat16),
            pltpu.SemaphoreType.DMA((levels, chunks)),
            pltpu.SemaphoreType.DMA((levels, chunks)),
        ],
        compiler_params=pltpu.CompilerParams(
            collective_id=1, has_side_effects=True, vmem_limit_bytes=40 << 20
        ),
        name="sum_rows",
    )(part)


def per_device(
    text_query, frame_key, frame_value, forward_out, out_grad, log_norms, lambdas, visits, bounds, text_count
):
    count = lax.axis_size("tokens")
    me = lax.axis_index("tokens")
    rows = text_query.shape[0]
    heads = lambdas.shape[0]
    value_size = frame_value.shape[1] // heads
    width = visits.shape[1] // 2

    grads = out_grad.astype(jnp.float32).reshape(rows, 1, heads, value_size)
    outs = forward_out.astype(jnp.float32).reshape(rows, 2, heads, value_size)
    coefs = jnp.stack([jnp.ones_like(lambdas), -lambdas])
    slopes = jnp.sum(grads * outs, axis=3) * coefs[None]
    mine = lax.dynamic_index_in_dim(visits, me, 0, keepdims=False)
    bound = lax.dynamic_index_in_dim(bounds, me, 0, keepdims=False)
    row_ids = jnp.arange(rows, dtype=jnp.int32)
    listed = jnp.where((row_ids >= bound)[:, None], mine[None, width:], mine[None, :width])
    hit = jnp.any(listed[:, :, None] == jnp.arange(count, dtype=jnp.int32)[None, None, :], axis=1)
    live = jnp.logical_and(hit, (me * rows + row_ids < text_count[0])[:, None]).astype(jnp.float32)
    lanes = -(-(4 * heads + count) // 128) * 128
    stats = jnp.concatenate(
        [
            log_norms.reshape(rows, 2 * heads) * LOG2E,
            slopes.reshape(rows, 2 * heads),
            live,
            jnp.zeros((rows, lanes - 4 * heads - count), jnp.float32),
        ],
        axis=1,
    )
    half = out_grad.shape[1] // 2
    sent = jnp.concatenate(
        [text_query.transpose(1, 0, 2), out_grad.reshape(rows, 2, half).transpose(1, 0, 2)], axis=0
    )
    all_rows, all_stats = gather_rows(count, sent, stats)
    part, key_grad, value_grad = heads_backward(
        all_rows, all_stats, frame_key.transpose(1, 0, 2), frame_value, lambdas
    )
    query_grad = sum_rows(part)
    return query_grad.transpose(1, 0, 2), key_grad.transpose(1, 0, 2), value_grad


def solution(mesh):
    both = ("groups", "tokens")
    return jax.shard_map(
        per_device,
        mesh=mesh,
        in_specs=(
            P(both, None, None),
            P(both, None, None),
            P(both, None),
            P(both, None, None),
            P(both, None),
            P(both, None, None),
            P(),
            P("groups", None),
            P("groups"),
            P(),
        ),
        out_specs=(P(both, None, None), P(both, None, None), P(both, None)),
        check_vma=False,
    )
```

```python
import functools
import math

import jax
import jax.numpy as jnp
from jax import lax
from jax.experimental import pallas as pl
from jax.experimental.pallas import tpu as pltpu
from jax.sharding import PartitionSpec as P

MESH = pl.DeviceIdType.MESH
LOG2E = math.log2(math.e)
VMEM = pl.BlockSpec(memory_space=pltpu.VMEM)


def place(levels):
    me = lax.axis_index("tokens")
    bits = [(me // 2**k) % 2 for k in range(levels)]
    position = sum(bits[k] * 2 ** (levels - 1 - k) for k in range(levels))
    partners = []
    for s in range(levels):
        step = 2 ** (levels - 1 - s)
        partners.append(me + step - 2 * step * bits[levels - 1 - s])
    return position, partners


def greet(partners):
    barrier = pltpu.get_barrier_semaphore()
    for partner in partners:
        pl.semaphore_signal(barrier, inc=1, device_id={"tokens": partner}, device_id_type=MESH)
    pl.semaphore_wait(barrier, len(partners))


def fused_kernel(
    levels,
    heads,
    lag,
    lambda_ref,
    visit_ref,
    bound_ref,
    count_ref,
    norm_ref,
    q_in,
    g_in,
    o_in,
    k_ref,
    v_ref,
    out_ref,
    dk_ref,
    dv_ref,
    rows_all,
    stat_all,
    stat_t,
    total,
    sending,
    landed,
    gather_send,
    gather_recv,
    stat_send,
    stat_recv,
    sum_send,
    sum_recv,
):
    step = pl.program_id(0)
    me = lax.axis_index("tokens")
    position, partners = place(levels)
    block_rows, key_size, value_size = q_in.shape[1], k_ref.shape[2], v_ref.shape[1]
    count = rows_all.shape[1]
    rows = count * block_rows
    scale = float(key_size) ** -0.5
    last = levels - 1
    warm = lag * levels

    def held(s):
        return pl.ds(position - position % 2**s, 2**s)

    def other(s):
        size = 2**s
        return pl.ds(position - position % size + size - 2 * size * ((position // size) % 2), size)

    def remote(s, source, target, send, recv):
        return pltpu.make_async_remote_copy(
            src_ref=source,
            dst_ref=target,
            send_sem=send,
            recv_sem=recv,
            device_id={"tokens": partners[s]},
            device_id_type=MESH,
        )

    def gather_copy(s, h, where):
        view = rows_all.at[h, where(s)]
        return remote(s, view, view, gather_send.at[s, h], gather_recv.at[s, h])

    def stat_copy(s, where):
        view = stat_all.at[where(s)]
        return remote(s, view, view, stat_send.at[s], stat_recv.at[s])

    def sum_copy(s, h):
        return remote(
            s, sending.at[h, other(s)], landed.at[h, pl.ds(2**s, 2**s)], sum_send.at[s, h], sum_recv.at[s, h]
        )

    @pl.when(step == 0)
    def _():
        greet(partners)
        for h in range(heads):
            keys = slice(h * key_size, (h + 1) * key_size)
            rows_all[h, position, :, 0:key_size] = q_in[0, :, keys]
            rows_all[h, position, :, key_size : 2 * key_size] = q_in[1, :, keys]
            rows_all[h, position, :, 2 * key_size :] = g_in[:, h * value_size : (h + 1) * value_size]
        lanes = lax.broadcasted_iota(jnp.int32, (block_rows, stat_all.shape[2]), 1)
        row_ids = lax.broadcasted_iota(jnp.int32, (block_rows, stat_all.shape[2]), 0)
        second = row_ids >= bound_ref[me]
        present = me * block_rows + row_ids < count_ref[0]
        width = visit_ref.shape[1] // 2
        stats = jnp.zeros((block_rows, stat_all.shape[2]), jnp.float32)
        for k in range(width):
            shard = jnp.where(second, visit_ref[me, width + k], visit_ref[me, k])
            stats = jnp.where(jnp.logical_and(lanes == 4 * heads + shard, present), 1.0, stats)
        stats = stats + norm_ref[...] * LOG2E
        for h in range(heads):
            values = slice(h * value_size, (h + 1) * value_size)
            g = g_in[:, values].astype(jnp.float32)
            for m in range(2):
                coef = 1.0 if m == 0 else -lambda_ref[h]
                slope = jnp.sum(g * o_in[m, :, values].astype(jnp.float32), axis=1, keepdims=True) * coef
                stats = jnp.where(lanes == (2 + m) * heads + h, slope, stats)
        stat_all[position] = stats

    for s in range(levels):
        h = step - lag * s

        @pl.when(jnp.logical_and(h >= 0, h < heads))
        def _():
            if s > 0:
                gather_copy(s - 1, h, other).wait_recv()
            gather_copy(s, h, held).start()

        @pl.when(h == 0)
        def _():
            if s > 0:
                stat_copy(s - 1, other).wait_recv()
            stat_copy(s, held).start()

    for s in range(last, -1, -1):
        h = step - warm - lag * (levels - s)

        @pl.when(jnp.logical_and(h >= 0, h < heads))
        def _():
            sum_copy(s, h).wait_recv()
            new = total[h, held(s)] + landed[h, pl.ds(2**s, 2**s)].astype(jnp.float32)
            if s > 0:
                total[h, held(s)] = new
                sending[h, other(s - 1)] = total[h, other(s - 1)].astype(sending.dtype)
                sum_copy(s - 1, h).start()
            else:
                out_ref[:, :, pl.ds(pl.multiple_of(h * key_size, key_size), key_size)] = new[0].astype(out_ref.dtype)

    head = step - warm

    @pl.when(head == 0)
    def _():
        stat_copy(last, other).wait_recv()
        stat_t[...] = stat_all[...].reshape(rows, stat_all.shape[2]).T

    @pl.when(jnp.logical_and(head >= 0, head < heads))
    def _():
        gather_copy(last, head, other).wait_recv()

        def flat(x):
            return x.astype(jnp.float32).reshape(rows, x.shape[2]).astype(jnp.bfloat16)

        def row(i):
            return stat_t[pl.ds(i, 1), :]

        def dot(a, b, dims):
            return lax.dot_general(a, b, (dims, ((), ())), preferred_element_type=jnp.float32)

        weight_two = lambda_ref[head]
        live = row(4 * heads + me)
        g = flat(rows_all[head, :, :, 2 * key_size :])
        spread = dot(v_ref[...], g, ((1,), (1,)))
        probs = []
        for m in range(2):
            q = flat(rows_all[head, :, :, m * key_size : (m + 1) * key_size])
            k = k_ref[m]
            score = dot(k, q, ((1,), (1,)))
            prob = live * jnp.exp2(score * (scale * LOG2E) - row(m * heads + head))
            coef_spread = spread if m == 0 else -weight_two * spread
            grad = (prob * (coef_spread - row((2 + m) * heads + head))).astype(jnp.bfloat16)
            probs.append(prob)
            dq = dot(grad, k, ((0,), (0,))) * scale
            total[head, :, m] = dq.reshape(count, block_rows, key_size)
            dk_ref[m] = (dot(grad, q, ((1,), (0,))) * scale).astype(jnp.bfloat16)
        sending[head, other(last)] = total[head, other(last)].astype(sending.dtype)
        sum_copy(last, head).start()
        mixed = (probs[0] - weight_two * probs[1]).astype(jnp.bfloat16)
        dv_ref[...] = dot(mixed, g, ((1,), (0,))).astype(jnp.bfloat16)

    @pl.when(step == pl.num_programs(0) - 1)
    def _():
        for s in range(levels):
            stat_copy(s, held).wait_send()

            @pl.loop(0, heads)
            def _(h):
                gather_copy(s, h, held).wait_send()
                sum_copy(s, h).wait_send()


def per_device(
    text_query, frame_key, frame_value, forward_out, out_grad, log_norms, lambdas, visits, bounds, text_count
):
    count = lax.axis_size("tokens")
    levels = count.bit_length() - 1
    lag = 1
    block_rows = text_query.shape[0]
    heads = lambdas.shape[0]
    frames = frame_key.shape[0]
    key_size, value_size = text_query.shape[2] // heads, frame_value.shape[1] // heads
    lanes = -(-(4 * heads + count) // 128) * 128
    norms = jnp.pad(log_norms.reshape(block_rows, 2 * heads), ((0, 0), (0, lanes - 2 * heads)))
    warm = lag * levels
    dma = pltpu.SemaphoreType.DMA
    smem = pl.BlockSpec(memory_space=pltpu.SMEM)

    def whole(shape):
        return pl.BlockSpec(shape, lambda j: (0,) * len(shape))

    def at(j):
        return jnp.clip(j - warm, 0, heads - 1)

    key_spec = pl.BlockSpec((2, frames, key_size), lambda j: (0, 0, at(j)))
    value_spec = pl.BlockSpec((frames, value_size), lambda j: (0, at(j)))
    queries = text_query.transpose(1, 0, 2)
    keys = frame_key.transpose(1, 0, 2)
    outs = forward_out.transpose(1, 0, 2)
    query_grad, key_grad, value_grad = pl.pallas_call(
        functools.partial(fused_kernel, levels, heads, lag),
        out_shape=(
            jax.ShapeDtypeStruct(queries.shape, jnp.bfloat16),
            jax.ShapeDtypeStruct(keys.shape, jnp.bfloat16),
            jax.ShapeDtypeStruct(frame_value.shape, jnp.bfloat16),
        ),
        grid=(heads + 2 * warm,),
        in_specs=[
            smem,
            smem,
            smem,
            smem,
            whole(norms.shape),
            whole(queries.shape),
            whole(out_grad.shape),
            whole(outs.shape),
            key_spec,
            value_spec,
        ],
        out_specs=(whole(queries.shape), key_spec, value_spec),
        scratch_shapes=[
            pltpu.VMEM((heads, count, block_rows, 2 * key_size + value_size), jnp.bfloat16),
            pltpu.VMEM((count, block_rows, lanes), jnp.float32),
            pltpu.VMEM((lanes, count * block_rows), jnp.float32),
            pltpu.VMEM((heads, count, 2, block_rows, key_size), jnp.float32),
            pltpu.VMEM((heads, count, 2, block_rows, key_size), jnp.bfloat16),
            pltpu.VMEM((heads, count, 2, block_rows, key_size), jnp.bfloat16),
            dma((levels, heads)),
            dma((levels, heads)),
            dma((levels,)),
            dma((levels,)),
            dma((levels, heads)),
            dma((levels, heads)),
        ],
        compiler_params=pltpu.CompilerParams(
            dimension_semantics=("arbitrary",),
            collective_id=0,
            has_side_effects=True,
            vmem_limit_bytes=48 << 20,
        ),
        name="fused_backward",
    )(lambdas, visits, bounds, text_count, norms, queries, out_grad, outs, keys, frame_value)
    return query_grad.transpose(1, 0, 2), key_grad.transpose(1, 0, 2), value_grad


def solution(mesh):
    both = ("groups", "tokens")
    return jax.shard_map(
        per_device,
        mesh=mesh,
        in_specs=(
            P(both, None, None),
            P(both, None, None),
            P(both, None),
            P(both, None, None),
            P(both, None),
            P(both, None, None),
            P(),
            P("groups", None),
            P("groups"),
            P(),
        ),
        out_specs=(P(both, None, None), P(both, None, None), P(both, None)),
        check_vma=False,
    )
```

```python
import functools
import math

import jax
import jax.numpy as jnp
from jax import lax
from jax.experimental import pallas as pl
from jax.experimental.pallas import tpu as pltpu
from jax.sharding import PartitionSpec as P

MESH = pl.DeviceIdType.MESH
LOG2E = math.log2(math.e)
VMEM = pl.BlockSpec(memory_space=pltpu.VMEM)


def radices_of(count):
    radices, left = [], count
    while left > 1:
        radix = 2 if len(radices) < 2 or left % 4 else 4
        radices.append(radix)
        left //= radix
    return tuple(reversed(radices))


def place(radices):
    me = lax.axis_index("tokens")
    stride = math.prod(radices)
    position, weight, digits, partners = 0, 1, [], []
    for radix in radices:
        stride //= radix
        digit = (me // stride) % radix
        digits.append(digit)
        partners.append([me + ((digit + r) % radix - digit) * stride for r in range(1, radix)])
        position = position + digit * weight
        weight *= radix
    return position, digits, partners


def greet(partners):
    barrier = pltpu.get_barrier_semaphore()
    partners = [p for group in partners for p in group]
    for partner in partners:
        pl.semaphore_signal(barrier, inc=1, device_id={"tokens": partner}, device_id_type=MESH)
    pl.semaphore_wait(barrier, len(partners))


def fused_kernel(
    radices,
    heads,
    chunks,
    lag,
    lambda_ref,
    visit_ref,
    bound_ref,
    count_ref,
    norm_ref,
    q_in,
    g_in,
    o_in,
    k_ref,
    v_ref,
    out_ref,
    dk_ref,
    dv_ref,
    rows_all,
    stat_all,
    stat_t,
    total,
    sending,
    landed,
    gather_send,
    gather_recv,
    stat_send,
    stat_recv,
    sum_send,
    sum_recv,
):
    step = pl.program_id(0)
    me = lax.axis_index("tokens")
    levels = len(radices)
    sizes = [math.prod(radices[:s]) for s in range(levels)]
    position, digits, partners = place(radices)
    per = heads // chunks
    block_rows, key_size, value_size = q_in.shape[1], k_ref.shape[2] // per, v_ref.shape[1] // per
    key_wide, value_wide = per * key_size, per * value_size
    count = rows_all.shape[1]
    rows = count * block_rows
    scale = float(key_size) ** -0.5
    last = levels - 1
    warm = lag * levels

    def held(s):
        return pl.ds(position - position % sizes[s], sizes[s])

    def part(s, r):
        size, radix = sizes[s], radices[s]
        return pl.ds(position - position % (size * radix) + (digits[s] + r + radix) % radix * size, size)

    def slot(s, r):
        return pl.ds(r * sizes[s], sizes[s])

    def hops(s):
        return range(1, radices[s])

    def remote(s, r, source, target, send, recv):
        return pltpu.make_async_remote_copy(
            src_ref=source,
            dst_ref=target,
            send_sem=send,
            recv_sem=recv,
            device_id={"tokens": partners[s][r - 1]},
            device_id_type=MESH,
        )

    def gather_copy(s, h, r, where):
        view = rows_all.at[h, where]
        return remote(s, r, view, view, gather_send.at[s, r, h], gather_recv.at[s, r, h])

    def stat_copy(s, r, where):
        view = stat_all.at[where]
        return remote(s, r, view, view, stat_send.at[s, r], stat_recv.at[s, r])

    def sum_copy(s, h, r):
        return remote(
            s, r, sending.at[h, part(s, r)], landed.at[h, slot(s, r)], sum_send.at[s, r, h], sum_recv.at[s, r, h]
        )

    def gather_arrived(s, h):
        for r in hops(s):
            gather_copy(s, h, r, part(s, -r)).wait_recv()

    def stats_arrived(s):
        for r in hops(s):
            stat_copy(s, r, part(s, -r)).wait_recv()

    def send_sums(s, h):
        for r in hops(s):
            away = part(s, r)
            sending[h, away] = total[h, away].astype(sending.dtype)
            sum_copy(s, h, r).start()

    @pl.when(step == 0)
    def _():
        greet(partners)
        for c in range(chunks):
            keys = slice(c * key_wide, (c + 1) * key_wide)
            rows_all[c, position, :, 0:key_wide] = q_in[0, :, keys]
            rows_all[c, position, :, key_wide : 2 * key_wide] = q_in[1, :, keys]
            rows_all[c, position, :, 2 * key_wide :] = g_in[:, c * value_wide : (c + 1) * value_wide]
        lanes = lax.broadcasted_iota(jnp.int32, (block_rows, stat_all.shape[2]), 1)
        row_ids = lax.broadcasted_iota(jnp.int32, (block_rows, stat_all.shape[2]), 0)
        second = row_ids >= bound_ref[me]
        present = me * block_rows + row_ids < count_ref[0]
        width = visit_ref.shape[1] // 2
        stats = jnp.zeros((block_rows, stat_all.shape[2]), jnp.float32)
        for k in range(width):
            shard = jnp.where(second, visit_ref[me, width + k], visit_ref[me, k])
            stats = jnp.where(jnp.logical_and(lanes == 4 * heads + shard, present), 1.0, stats)
        stats = stats + norm_ref[...] * LOG2E
        for h in range(heads):
            values = slice(h * value_size, (h + 1) * value_size)
            g = g_in[:, values].astype(jnp.float32)
            for m in range(2):
                coef = 1.0 if m == 0 else -lambda_ref[h]
                slope = jnp.sum(g * o_in[m, :, values].astype(jnp.float32), axis=1, keepdims=True) * coef
                stats = jnp.where(lanes == (2 + m) * heads + h, slope, stats)
        stat_all[position] = stats

    for s in range(levels):
        h = step - lag * s

        @pl.when(jnp.logical_and(h >= 0, h < chunks))
        def _():
            if s > 0:
                gather_arrived(s - 1, h)
            for r in hops(s):
                gather_copy(s, h, r, held(s)).start()

        @pl.when(h == 0)
        def _():
            if s > 0:
                stats_arrived(s - 1)
            for r in hops(s):
                stat_copy(s, r, held(s)).start()

    for s in range(last, -1, -1):
        h = step - warm - lag * (levels - s)

        @pl.when(jnp.logical_and(h >= 0, h < chunks))
        def _():
            new = total[h, held(s)]
            for r in hops(s):
                sum_copy(s, h, r).wait_recv()
                new = new + landed[h, slot(s, r)].astype(jnp.float32)
            if s > 0:
                total[h, held(s)] = new
                send_sums(s - 1, h)
            else:
                out_ref[:, :, pl.ds(pl.multiple_of(h * key_wide, key_wide), key_wide)] = new[0].astype(out_ref.dtype)

    chunk = step - warm

    @pl.when(chunk == 0)
    def _():
        stats_arrived(last)
        stat_t[...] = stat_all[...].reshape(rows, stat_all.shape[2]).T

    @pl.when(jnp.logical_and(chunk >= 0, chunk < chunks))
    def _():
        gather_arrived(last, chunk)

        def flat(x):
            return x.astype(jnp.float32).reshape(rows, x.shape[2]).astype(jnp.bfloat16)

        def row(i):
            return stat_t[pl.ds(i, 1), :]

        def dot(a, b, dims):
            return lax.dot_general(a, b, (dims, ((), ())), preferred_element_type=jnp.float32)

        live = row(4 * heads + me)
        for i in range(per):
            head = chunk * per + i
            weight_two = lambda_ref[head]
            keys = slice(i * key_size, (i + 1) * key_size)
            values = slice(i * value_size, (i + 1) * value_size)
            g = flat(rows_all[chunk, :, :, 2 * key_wide + i * value_size : 2 * key_wide + (i + 1) * value_size])
            spread = dot(v_ref[:, values], g, ((1,), (1,)))
            probs = []
            for m in range(2):
                first = m * key_wide + i * key_size
                q = flat(rows_all[chunk, :, :, first : first + key_size])
                k = k_ref[m, :, keys]
                score = dot(k, q, ((1,), (1,)))
                prob = live * jnp.exp2(score * (scale * LOG2E) - row(m * heads + head))
                coef_spread = spread if m == 0 else -weight_two * spread
                grad = (prob * (coef_spread - row((2 + m) * heads + head))).astype(jnp.bfloat16)
                probs.append(prob)
                dq = dot(grad, k, ((0,), (0,))) * scale
                total[chunk, :, m, :, keys] = dq.reshape(count, block_rows, key_size)
                dk_ref[m, :, keys] = (dot(grad, q, ((1,), (0,))) * scale).astype(jnp.bfloat16)
            mixed = (probs[0] - weight_two * probs[1]).astype(jnp.bfloat16)
            dv_ref[:, values] = dot(mixed, g, ((1,), (0,))).astype(jnp.bfloat16)
        send_sums(last, chunk)

    @pl.when(step == pl.num_programs(0) - 1)
    def _():
        for s in range(levels):
            for r in hops(s):
                stat_copy(s, r, held(s)).wait_send()

                @pl.loop(0, chunks)
                def _(h):
                    gather_copy(s, h, r, held(s)).wait_send()
                    sum_copy(s, h, r).wait_send()


def per_device(
    text_query, frame_key, frame_value, forward_out, out_grad, log_norms, lambdas, visits, bounds, text_count
):
    count = lax.axis_size("tokens")
    radices = radices_of(count)
    levels, widest = len(radices), max(radices)
    lag = 1
    block_rows = text_query.shape[0]
    heads = lambdas.shape[0]
    chunks = heads // 2 if heads % 2 == 0 else heads
    frames = frame_key.shape[0]
    key_size, value_size = text_query.shape[2] // heads, frame_value.shape[1] // heads
    key_wide, value_wide = key_size * heads // chunks, value_size * heads // chunks
    lanes = -(-(4 * heads + count) // 128) * 128
    norms = jnp.pad(log_norms.reshape(block_rows, 2 * heads), ((0, 0), (0, lanes - 2 * heads)))
    warm = lag * levels
    dma = pltpu.SemaphoreType.DMA
    smem = pl.BlockSpec(memory_space=pltpu.SMEM)

    def whole(shape):
        return pl.BlockSpec(shape, lambda j: (0,) * len(shape))

    def at(j):
        return jnp.clip(j - warm, 0, chunks - 1)

    key_spec = pl.BlockSpec((2, frames, key_wide), lambda j: (0, 0, at(j)))
    value_spec = pl.BlockSpec((frames, value_wide), lambda j: (0, at(j)))
    queries = text_query.transpose(1, 0, 2)
    keys = frame_key.transpose(1, 0, 2)
    outs = forward_out.transpose(1, 0, 2)
    query_grad, key_grad, value_grad = pl.pallas_call(
        functools.partial(fused_kernel, radices, heads, chunks, lag),
        out_shape=(
            jax.ShapeDtypeStruct(queries.shape, jnp.bfloat16),
            jax.ShapeDtypeStruct(keys.shape, jnp.bfloat16),
            jax.ShapeDtypeStruct(frame_value.shape, jnp.bfloat16),
        ),
        grid=(chunks + 2 * warm,),
        in_specs=[
            smem,
            smem,
            smem,
            smem,
            whole(norms.shape),
            whole(queries.shape),
            whole(out_grad.shape),
            whole(outs.shape),
            key_spec,
            value_spec,
        ],
        out_specs=(whole(queries.shape), key_spec, value_spec),
        scratch_shapes=[
            pltpu.VMEM((chunks, count, block_rows, 2 * key_wide + value_wide), jnp.bfloat16),
            pltpu.VMEM((count, block_rows, lanes), jnp.float32),
            pltpu.VMEM((lanes, count * block_rows), jnp.float32),
            pltpu.VMEM((chunks, count, 2, block_rows, key_wide), jnp.float32),
            pltpu.VMEM((chunks, count, 2, block_rows, key_wide), jnp.bfloat16),
            pltpu.VMEM((chunks, count, 2, block_rows, key_wide), jnp.bfloat16),
            dma((levels, widest, chunks)),
            dma((levels, widest, chunks)),
            dma((levels, widest)),
            dma((levels, widest)),
            dma((levels, widest, chunks)),
            dma((levels, widest, chunks)),
        ],
        compiler_params=pltpu.CompilerParams(
            dimension_semantics=("arbitrary",),
            collective_id=0,
            has_side_effects=True,
            vmem_limit_bytes=48 << 20,
        ),
        name="fused_backward",
    )(lambdas, visits, bounds, text_count, norms, queries, out_grad, outs, keys, frame_value)
    return query_grad.transpose(1, 0, 2), key_grad.transpose(1, 0, 2), value_grad


def solution(mesh):
    both = ("groups", "tokens")
    return jax.shard_map(
        per_device,
        mesh=mesh,
        in_specs=(
            P(both, None, None),
            P(both, None, None),
            P(both, None),
            P(both, None, None),
            P(both, None),
            P(both, None, None),
            P(),
            P("groups", None),
            P("groups"),
            P(),
        ),
        out_specs=(P(both, None, None), P(both, None, None), P(both, None)),
        check_vma=False,
    )
```
